32 devices in a mesh: groups: 2 (over x), expert: 16 (over z, y, core).
Axes of the slice: x: 2, y: 2, z: 4, core: 2. Of those that a mesh axis runs over, the one named last changes fastest.
Arguments:
- hidden_in: bfloat16 [4096, 2048], P(('groups', 'expert')), parts along dimension 0, may hold values from -6 to 6
- norm_gain: float32 [2048], replicated, may hold values from 0.1 to 1.9
- router_weight: bfloat16 [2048, 16], replicated, may hold values from -0.125 to 0.125
- expert_ids: int32 [4096, 8], P(('groups', 'expert')), parts along dimension 0, may hold values from 0 to 15, all different within a row; in each aligned block of 128 rows (0 to 127, 128 to 255, ...) at most 96 rows name the same one
- w_gate: bfloat16 [16, 2048, 768], P('expert'), may hold values from -0.125 to 0.125
- w_up: bfloat16 [16, 2048, 768], P('expert'), may hold values from -0.125 to 0.125
- w_down: bfloat16 [16, 768, 2048], P('expert'), may hold values from -0.21875 to 0.21875
Outputs:
- combined: bfloat16 [4096, 2048], P(('groups', 'expert')), parts along dimension 0
The draws below stay inside these ranges and needn't reach their ends.
There are 2 independent parts, one for each index of `groups`. The reference program is written for one: setup_inputs(seed, part) draws one part's arguments, and reference() takes and returns one part's arrays. A program takes and returns all parts, laid end to end along the dimension named above; an argument that names none is the same for every part. Nothing has to cross between parts.
Inputs may be any that keep to these rules, and one draw needn't show every extreme that they name: `expert_ids`: each row names 8 different experts; within each aligned block of 128 rows (the rows of one device) no expert is named by more than 96 rows, a bound that some block reaches.
All inputs are finite; a program needn't handle non-finite values.
Results may differ from the reference program's by a relative error of at most 0.0074.
Values may be sent and summed in bfloat16 or wider, within the bound.
A program may use at most 128 MiB of HBM per device.

```python
import math
import jax
import jax.numpy as jnp
import numpy as np
from jax import lax

D = 2048
FF = 768
TOP = 8
TOK_DEV = 128
EXPERTS = 16
CAP = 96
TOKENS = 2048


def shard_levels(rng, shape, pieces, smallest, largest):
    gain = 1.0
    for axis_at, shards_of in pieces:
        heights = jax.random.uniform(jax.random.fold_in(jax.random.fold_in(rng, 6), axis_at), (shards_of,), jnp.float32, smallest / len(pieces), largest / len(pieces))
        gain = gain * jnp.repeat(jnp.exp(heights), shape[axis_at] // shards_of).reshape((-1,) + (1,) * (len(shape) - 1 - axis_at))
    return gain


def assign_block(own_key, own, number, rows, count, top, reach, skew):
    sequence = jax.random.permutation(own_key, count)
    crowded, common = shares(count, rows * top, reach, skew, True), shares(count, rows * top, reach, skew, False)
    places = jnp.arange(count)

    def named(lengths, offset_by):
        used = int((lengths > 0).sum())
        fixed = max(1, used // 4)
        passed = fixed + (places - fixed + offset_by * (used - fixed)) % max(1, count - fixed)
        return jnp.zeros((count,), jnp.int32).at[sequence[jnp.where(places < fixed, places, passed)]].set(jnp.asarray(lengths, jnp.int32))

    lengths = jnp.where(number % 4 == 0, named(crowded, number // 4), named(common, number - number // 4 - 1))
    mixed = jax.random.permutation(jax.random.fold_in(own, 3), count)
    donor, receiver = mixed[0:count // 2 * 2:2], mixed[1:count // 2 * 2:2]
    margin = jnp.minimum(lengths[donor] - 1, reach - lengths[receiver]) // 2
    margin = jnp.where((donor == sequence[0]) | (receiver == sequence[0]) | (lengths[receiver] == 0), 0, jnp.maximum(margin, 0))
    passed = jax.random.randint(jax.random.fold_in(own, 4), (count // 2,), 0, 1 << 20) % (margin + 1)
    lengths = lengths.at[donor].add(-passed).at[receiver].add(passed)
    items = jnp.searchsorted(jnp.cumsum(lengths), jnp.arange(rows * top), side="right").astype(jnp.int32)
    table = items.reshape(top, rows).T
    table = table[jax.random.permutation(jax.random.fold_in(own, 1), rows)]
    offset_by = jax.random.randint(jax.random.fold_in(own, 2), (rows, 1), 0, top)
    return jnp.take_along_axis(table, (jnp.arange(top)[None, :] + offset_by) % top, axis=1)


def shares(count, total, bound, slope, full):
    loads = [(1 << 20) // math.isqrt(grade ** slope) + 1 for grade in range(1, count + 1)]
    largest = bound if full else min(bound, max(-(-total // count), total * loads[0] // sum(loads)))
    least = 1 if total - largest >= count - 1 else 0
    holding, spare = [largest] + [least] * (count - 1), total - largest - least * (count - 1)
    while spare > 0:
        free = [i for i in range(1, count) if holding[i] < largest] or [i for i in range(1, count) if holding[i] < bound]
        mass, left = sum([loads[i] for i in free]), spare
        for i in free:
            more = min(bound - holding[i], max(1, left * loads[i] // mass), spare)
            holding[i] = holding[i] + more
            spare = spare - more
    return np.array(holding)


def normal_values(own_key, shape, spread, bound, split=(), held_as=jnp.bfloat16):
    values = spread * jax.random.normal(own_key, shape, jnp.float32)
    if split:
        values = values * shard_levels(own_key, shape, split, -0.22, 0.18)
    return jnp.clip(values, -bound, bound).astype(held_as)


def setup_inputs(seed: int = 0, part: int = 0) -> dict:
    key_of = jax.random.split(jax.random.key(seed), 8)
    part_splits = jax.random.split(jax.random.fold_in(key_of[7], part), 8)
    hidden_in = normal_values(part_splits[0], (TOKENS, D), 1.0, 6.0, ((0, 16),))
    norm_gain = jnp.clip(1.0 + 0.18 * jax.random.normal(key_of[1], (D,), jnp.float32), 0.1, 1.9)
    router_weight = normal_values(key_of[2], (D, EXPERTS), D ** -0.5, 0.125)
    expert_ids_keys = jax.random.split(jax.random.fold_in(part_splits[3], 1), TOKENS // TOK_DEV)
    expert_ids_turns = jax.random.permutation(jax.random.fold_in(part_splits[3], 3), TOKENS // TOK_DEV)
    expert_ids = jax.vmap(lambda own, number: assign_block(jax.random.fold_in(part_splits[3], 2), own, number, TOK_DEV, EXPERTS, TOP, CAP, 2))(expert_ids_keys, expert_ids_turns).reshape((TOKENS, TOP))
    w_gate = normal_values(key_of[4], (EXPERTS, D, FF), D ** -0.5, 0.125, ((0, 16),))
    w_up = normal_values(key_of[5], (EXPERTS, D, FF), D ** -0.5, 0.125, ((0, 16),))
    w_down = normal_values(key_of[6], (EXPERTS, FF, D), FF ** -0.5, 0.21875, ((0, 16),))
    return {"hidden_in": hidden_in, "norm_gain": norm_gain, "router_weight": router_weight, "expert_ids": expert_ids, "w_gate": w_gate, "w_up": w_up, "w_down": w_down}


def expert_mlp(item):
    rows, gate_w, up_w, down_w = item
    gate_act = jnp.dot(rows, gate_w, preferred_element_type=jnp.float32)
    up_act = jnp.dot(rows, up_w, preferred_element_type=jnp.float32)
    hidden = (jax.nn.silu(gate_act) * up_act).astype(jnp.bfloat16)
    return jnp.dot(hidden, down_w, preferred_element_type=jnp.float32).astype(jnp.bfloat16)

def reference(hidden_in, norm_gain, router_weight, expert_ids, w_gate, w_up, w_down):
    as_float = hidden_in.astype(jnp.float32)
    inv_rms = lax.rsqrt(lax.optimization_barrier(jnp.mean(as_float * as_float, axis=1, keepdims=True)) + 1e-06)
    normed = (as_float * inv_rms * norm_gain).astype(jnp.bfloat16)
    logits = jnp.dot(normed, router_weight, preferred_element_type=jnp.float32)
    exp_logits = jnp.exp(logits)
    picked = jnp.take_along_axis(exp_logits, expert_ids, axis=1)
    route_w = picked / lax.optimization_barrier(jnp.sum(picked, axis=1, keepdims=True))
    blocks = TOKENS // TOK_DEV
    flat_ids = expert_ids.reshape(blocks, TOK_DEV * TOP).astype(jnp.int32)
    onehot = (flat_ids[:, :, None] == jnp.arange(EXPERTS, dtype=jnp.int32)[None, None, :]).astype(jnp.int32)
    before = jnp.cumsum(onehot, axis=1) - onehot
    slot_index = lax.optimization_barrier(jnp.sum(before * onehot, axis=2)).astype(jnp.int32)
    block_index = jnp.arange(blocks, dtype=jnp.int32)[:, None]
    dest_index = (flat_ids * (blocks * CAP) + block_index * CAP + slot_index).reshape(-1).astype(jnp.int32)
    token_rows = jnp.repeat(normed, TOP, axis=0)
    packed = jnp.zeros((EXPERTS * blocks * CAP, D), jnp.bfloat16).at[dest_index].set(token_rows)
    packed = packed.reshape(EXPERTS, blocks * CAP, D)
    expert_out = lax.map(expert_mlp, (packed, w_gate, w_up, w_down)).reshape(EXPERTS * blocks * CAP, D)
    gathered = expert_out[dest_index].reshape(TOKENS, TOP, D)
    combined = lax.optimization_barrier(jnp.sum(gathered.astype(jnp.float32) * route_w[:, :, None], axis=1)).astype(jnp.bfloat16)
    return combined
```

```python
import jax
import jax.numpy as jnp
from jax import lax
from jax.experimental import pallas as pl
from jax.experimental.pallas import tpu as pltpu
from jax.sharding import PartitionSpec as P

RING = 8
PLACE = {0: 0, 1: 1, 7: 2, 2: 3, 6: 4, 3: 5, 5: 6, 4: 7}
OFFSET_AT = {place: offset for offset, place in PLACE.items()}


def ring_kernel(
    x_ref, gain_ref, router_ref, ids_ref, gate_hbm, up_hbm, down_hbm, out_ref,
    gate_w, up_w, down_w, xg, yb, ys, from_left, from_right, hb, route_out, route_in, route_col,
    load_sem, ag_s, ag_r, sx_s, sx_r, sy_s, sy_r, rs_s, rs_r, w_s, w_r,
):
    count = 2 * RING
    rows = x_ref.shape[0]
    width = x_ref.shape[1]
    ff = gate_w.shape[1]
    me = lax.axis_index("expert")
    core = me % 2
    y_at = (me // 2) % 2
    z_at = me // 4
    place = z_at * (1 - y_at) + (RING - 1 - z_at) * y_at

    def device_at(ring_place, which_core):
        high = ring_place // 4
        depth = ring_place * (1 - high) + (RING - 1 - ring_place) * high
        return (depth * 2 + high) * 2 + which_core

    right = device_at((place + 1) % RING, core)
    left = device_at((place + RING - 1) % RING, core)
    sibling = me + 1 - 2 * core

    loads = [
        pltpu.make_async_copy(src.at[0], dst, load_sem.at[i])
        for i, (src, dst) in enumerate(((gate_hbm, gate_w), (up_hbm, up_w), (down_hbm, down_w)))
    ]
    for load in loads:
        load.start()

    barrier = pltpu.get_barrier_semaphore()

    @pl.loop(1, count)
    def _(step):
        pl.semaphore_signal(
            barrier, inc=1, device_id={"expert": (me + step) % count},
            device_id_type=pl.DeviceIdType.MESH,
        )

    def remote(src, dst, send, recv, device):
        return pltpu.make_async_remote_copy(
            src_ref=src, dst_ref=dst, send_sem=send, recv_sem=recv,
            device_id={"expert": device}, device_id_type=pl.DeviceIdType.MESH,
        )

    as_float = x_ref[...].astype(jnp.float32)
    inv_rms = lax.rsqrt(jnp.mean(as_float * as_float, axis=1, keepdims=True) + 1e-06)
    normed = (as_float * inv_rms * gain_ref[...]).astype(jnp.bfloat16)
    xg[0, 0] = normed.reshape(2, rows // 2, width)
    pl.semaphore_wait(barrier, count - 1)

    def gather_copy(way, step):
        if way == 0:
            src, dst, device = PLACE[step], PLACE[step + 1], right
        else:
            src, dst, device = PLACE[(RING - step) % RING], PLACE[RING - 1 - step], left
        if step < 3:
            src_ref, dst_ref = xg.at[src, 0], xg.at[dst, 0]
        else:
            src_ref, dst_ref = xg.at[src, 0, way], xg.at[dst, 0, way]
        return remote(src_ref, dst_ref, ag_s.at[way, step], ag_r.at[way, step], device)

    def sibling_x(offset):
        at = PLACE[offset]
        return remote(xg.at[at, 0], xg.at[at, 1], sx_s.at[at], sx_r.at[at], sibling)

    def sibling_y(offset):
        at = PLACE[offset]
        return remote(yb.at[at, 1], ys.at[at], sy_s.at[at], sy_r.at[at], sibling)

    gather_copy(0, 0).start()
    gather_copy(1, 0).start()
    sibling_x(0).start()

    logits = lax.dot_general(
        router_ref[...], normed, (((1,), (1,)), ((), ())), preferred_element_type=jnp.float32
    )
    exp_logits = jnp.exp(logits)
    expert_iota = lax.broadcasted_iota(jnp.int32, logits.shape, 0)
    chosen = expert_iota < 0
    for k in range(ids_ref.shape[0]):
        chosen = chosen | (ids_ref[k : k + 1, :] == expert_iota)
    picked = jnp.where(chosen, exp_logits, 0.0)
    route = picked / jnp.sum(picked, axis=0, keepdims=True)
    for e in range(count):
        route_out[e] = jnp.broadcast_to(route[e : e + 1, :], (8, rows))

    def route_copy(step):
        peer = (me + step) % count
        return remote(route_out.at[peer], route_in.at[step], w_s.at[step], w_r.at[step], peer)

    @pl.loop(1, count)
    def _(step):
        route_copy(step).start()

    route_in[0] = route_out[me]

    @pl.loop(1, count)
    def _(step):
        route_copy(step).wait_recv()

    diagonal = lax.broadcasted_iota(jnp.int32, (rows, rows), 0) == lax.broadcasted_iota(
        jnp.int32, (rows, rows), 1
    )
    for at in range(RING):
        for lane in range(2):
            source = device_at((place + RING - OFFSET_AT[at]) % RING, core + lane - 2 * core * lane)
            values = route_in[(me + count - source) % count]
            column = jnp.sum(jnp.where(diagonal, values[0:1, :], 0.0), axis=1, keepdims=True)
            route_col[at, lane] = jnp.broadcast_to(column, (rows, rows))

    def compute(at, blocks):
        total = blocks * 2 * rows

        @pl.loop(0, ff // 256)
        def _(tile):
            columns = pl.ds(pl.multiple_of(tile * 256, 256), 256)
            x = xg[at : at + blocks].reshape(total, width)
            gate = jnp.dot(x, gate_w[:, columns], preferred_element_type=jnp.float32)
            up = jnp.dot(x, up_w[:, columns], preferred_element_type=jnp.float32)
            hb[0:total, columns] = (gate / (1.0 + jnp.exp(-gate)) * up).astype(jnp.bfloat16)

        @pl.loop(0, width // 256)
        def _(tile):
            columns = pl.ds(pl.multiple_of(tile * 256, 256), 256)
            y = jnp.dot(hb[0:total, :], down_w[:, columns], preferred_element_type=jnp.float32)
            for block in range(blocks):
                for lane in range(2):
                    first = (block * 2 + lane) * rows
                    weight = route_col[at + block, lane]
                    weight = jnp.concatenate([weight, weight], axis=1)
                    part = (y[first : first + rows] * weight).astype(jnp.bfloat16)
                    yb[at + block, lane, :, :, columns] = part.reshape(2, rows // 2, 256)

    for load in loads:
        load.wait()
    sibling_x(0).wait_recv()
    compute(0, 1)
    sibling_y(0).start()

    for step in range(3):
        for way, offset in ((0, step + 1), (1, RING - 1 - step)):
            gather_copy(way, step).wait_recv()
            gather_copy(way, step + 1).start()
            sibling_x(offset).start()
        for offset in (step + 1, RING - 1 - step):
            sibling_x(offset).wait_recv()
        compute(2 * step + 1, 2)
        for offset in (step + 1, RING - 1 - step):
            sibling_y(offset).start()

    gather_copy(0, 3).wait_recv()
    gather_copy(1, 3).wait_recv()
    sibling_x(4).start()

    incoming = (from_left, from_right)

    def reduce_copy(way, half, hops):
        at = PLACE[RING - hops if way == 0 else hops]
        into = incoming[way]
        number = hops * 2 + half
        return remote(
            yb.at[at, 0, half], into.at[hops - 1, half],
            rs_s.at[way, number], rs_r.at[way, number], right if way == 0 else left,
        )

    def own_sum(at, half):
        return yb[at, 0, half].astype(jnp.float32) + ys[at, half].astype(jnp.float32)

    def reduce_start(way, half, hops, arrived):
        at = PLACE[RING - hops if way == 0 else hops]
        total = own_sum(at, half)
        if arrived:
            reduce_copy(way, half, hops + 1).wait_recv()
            total = total + incoming[way][hops, half].astype(jnp.float32)
        yb[at, 0, half] = total.astype(jnp.bfloat16)
        reduce_copy(way, half, hops).start()

    sibling_y(5).wait_recv()
    reduce_start(0, 1, 3, False)
    sibling_y(3).wait_recv()
    reduce_start(1, 0, 3, False)
    sibling_x(4).wait_recv()
    compute(7, 1)
    sibling_y(4).start()
    for offset in (0, 1, 2, 6, 7, 4):
        sibling_y(offset).wait_recv()
    reduce_start(0, 0, 4, False)
    reduce_start(1, 1, 4, False)
    for late, hops in ((0, 2), (1, 3), (0, 1), (1, 2), (1, 1)):
        reduce_start(0, 1 - late, hops, True)
        reduce_start(1, late, hops, True)
    for half in range(2):
        total = own_sum(0, half)
        for way in range(2):
            reduce_copy(way, half, 1).wait_recv()
            total = total + incoming[way][0, half].astype(jnp.float32)
        out_ref[half * (rows // 2) : (half + 1) * (rows // 2), :] = total.astype(jnp.bfloat16)

    for way in range(2):
        for step in range(4):
            gather_copy(way, step).wait_send()
        for hops in (1, 2, 3):
            for half in range(2):
                reduce_copy(way, half, hops).wait_send()
        reduce_copy(way, way, 4).wait_send()
    for offset in range(RING):
        sibling_x(offset).wait_send()
        sibling_y(offset).wait_send()

    @pl.loop(1, count)
    def _(step):
        route_copy(step).wait_send()


def ring_local(hidden_in, norm_gain, router_weight, expert_ids, w_gate, w_up, w_down):
    rows, width = hidden_in.shape
    ff = w_gate.shape[2]
    half = rows // 2
    vmem = pl.BlockSpec(memory_space=pltpu.VMEM)
    hbm = pl.BlockSpec(memory_space=pl.ANY)
    dma = pltpu.SemaphoreType.DMA
    return pl.pallas_call(
        ring_kernel,
        out_shape=jax.ShapeDtypeStruct((rows, width), jnp.bfloat16),
        in_specs=[vmem, vmem, vmem, vmem, hbm, hbm, hbm],
        out_specs=vmem,
        scratch_shapes=[
            pltpu.VMEM((width, ff), jnp.bfloat16),
            pltpu.VMEM((width, ff), jnp.bfloat16),
            pltpu.VMEM((ff, width), jnp.bfloat16),
            pltpu.VMEM((RING, 2, 2, half, width), jnp.bfloat16),
            pltpu.VMEM((RING, 2, 2, half, width), jnp.bfloat16),
            pltpu.VMEM((RING, 2, half, width), jnp.bfloat16),
            pltpu.VMEM((4, 2, half, width), jnp.bfloat16),
            pltpu.VMEM((4, 2, half, width), jnp.bfloat16),
            pltpu.VMEM((4 * rows, ff), jnp.bfloat16),
            pltpu.VMEM((2 * RING, 8, rows), jnp.float32),
            pltpu.VMEM((2 * RING, 8, rows), jnp.float32),
            pltpu.VMEM((RING, 2, rows, rows), jnp.float32),
            dma((3,)), dma((2, 4)), dma((2, 4)), dma((RING,)), dma((RING,)), dma((RING,)),
            dma((RING,)), dma((2, 10)), dma((2, 10)), dma((2 * RING,)), dma((2 * RING,)),
        ],
        compiler_params=pltpu.CompilerParams(
            collective_id=0, has_side_effects=True, vmem_limit_bytes=56 * 1024 * 1024
        ),
    )(hidden_in, norm_gain.reshape(1, width), router_weight.T, expert_ids.T, w_gate, w_up, w_down)


def local(hidden_in, norm_gain, router_weight, expert_ids, w_gate, w_up, w_down):
    tok_rows = hidden_in.shape[0]
    top_count = expert_ids.shape[1]
    num_experts = router_weight.shape[1]
    dev_count = lax.axis_size("expert")
    local_experts = w_gate.shape[0]
    cap_rows = tok_rows * top_count * 3 // (2 * num_experts)
    as_float = hidden_in.astype(jnp.float32)
    inv_rms = lax.rsqrt(jnp.mean(as_float * as_float, axis=1, keepdims=True) + 1e-06)
    normed = (as_float * inv_rms * norm_gain).astype(jnp.bfloat16)
    logits = jnp.dot(normed, router_weight, preferred_element_type=jnp.float32)
    exp_logits = jnp.exp(logits)
    expert_iota = jnp.arange(num_experts, dtype=jnp.int32)
    choice_hot = (expert_ids[:, :, None] == expert_iota[None, None, :]).astype(jnp.float32)
    picked = jnp.sum(choice_hot * exp_logits[:, None, :], axis=2)
    route_w = picked / jnp.sum(picked, axis=1, keepdims=True)
    flat_ids = expert_ids.reshape(-1)
    onehot = (flat_ids[:, None] == expert_iota[None, :]).astype(jnp.int32)
    before = jnp.cumsum(onehot, axis=0) - onehot
    slot_index = jnp.sum(before * onehot, axis=1)
    dest_index = (
        flat_ids // local_experts * cap_rows + slot_index
    ) * local_experts + flat_ids % local_experts
    token_rows = jnp.repeat(normed, top_count, axis=0)
    outgoing = (
        jnp.zeros((num_experts * cap_rows, normed.shape[1]), jnp.bfloat16)
        .at[dest_index]
        .set(token_rows)
    )
    outgoing = outgoing.reshape(dev_count, cap_rows, local_experts, normed.shape[1])
    arrived = lax.all_to_all(outgoing, "expert", split_axis=0, concat_axis=0, tiled=True)
    gate_act = jnp.einsum("smed,edf->smef", arrived, w_gate, preferred_element_type=jnp.float32)
    up_act = jnp.einsum("smed,edf->smef", arrived, w_up, preferred_element_type=jnp.float32)
    hidden = (jax.nn.silu(gate_act) * up_act).astype(jnp.bfloat16)
    returned = lax.all_to_all(
        jnp.einsum("smef,efd->smed", hidden, w_down, preferred_element_type=jnp.float32).astype(
            jnp.bfloat16
        ),
        "expert",
        split_axis=0,
        concat_axis=0,
        tiled=True,
    )
    returned = returned.reshape(num_experts * cap_rows, normed.shape[1])
    gathered = returned[dest_index].reshape(tok_rows, top_count, normed.shape[1])
    combined = jnp.sum(gathered.astype(jnp.float32) * route_w[:, :, None], axis=1).astype(
        jnp.bfloat16
    )
    return combined


def solution(mesh):
    in_specs = (
        P(("groups", "expert"), None),
        P(),
        P(),
        P(("groups", "expert"), None),
        P("expert", None, None),
        P("expert", None, None),
        P("expert", None, None),
    )
    out_specs = P(("groups", "expert"), None)
    ringed = mesh.shape["expert"] == 2 * RING
    body = ring_local if ringed else local
    return jax.shard_map(body, mesh=mesh, in_specs=in_specs, out_specs=out_specs, check_vma=False)
```

```python
import jax
import jax.numpy as jnp
from jax import lax
from jax.experimental import pallas as pl
from jax.experimental.pallas import tpu as pltpu
from jax.sharding import PartitionSpec as P

RING = 8
FF_TILE = 768
OUT_TILE = 1024


def spot(offset, half):
    if offset == 0:
        return 0, half
    if offset == 4:
        return 7, half
    if offset < 4:
        return 2 * offset - 1 + half, 0
    return 2 * (RING - offset) - half, 1


def ring_kernel(
    x_ref, gain_ref, router_ref, ids_ref, gate_hbm, up_hbm, down_hbm, out_ref,
    gate_w, up_w, down_w, xg, yb, ys, from_left, from_right, hb, routes, route_col, out_buf,
    load_sem, ag_s, ag_r, sx_s, sx_r, sy_s, sy_r, rs_s, rs_r, rt_s, rt_r, rx_s, rx_r, out_sem,
):
    rows = x_ref.shape[0]
    width = x_ref.shape[1]
    ff = gate_w.shape[1]
    half_rows = rows // 2
    total = 2 * rows
    me = lax.axis_index("expert")
    core = me % 2
    y_at = (me // 2) % 2
    z_at = me // 4
    place = z_at * (1 - y_at) + (RING - 1 - z_at) * y_at

    def device_at(ring_place):
        high = ring_place // 4
        depth = ring_place * (1 - high) + (RING - 1 - ring_place) * high
        return (depth * 2 + high) * 2 + core

    right = device_at((place + 1) % RING)
    left = device_at((place + RING - 1) % RING)
    sibling = me + 1 - 2 * core
    toward = (right, left)

    barrier = pltpu.get_barrier_semaphore()
    for device in (right, left, sibling):
        pl.semaphore_signal(
            barrier, inc=1, device_id={"expert": device}, device_id_type=pl.DeviceIdType.MESH
        )

    loads = [
        pltpu.make_async_copy(src.at[0], dst, load_sem.at[i])
        for i, (src, dst) in enumerate(((gate_hbm, gate_w), (up_hbm, up_w), (down_hbm, down_w)))
    ]
    for load in loads:
        load.start()

    def remote(src, dst, send, recv, device):
        return pltpu.make_async_remote_copy(
            src_ref=src, dst_ref=dst, send_sem=send, recv_sem=recv,
            device_id={"expert": device}, device_id_type=pl.DeviceIdType.MESH,
        )

    def offset_of(way, hop):
        return hop if way == 0 else (RING - hop) % RING

    def gather_copy(way, hop, late):
        half = late if way == 0 else 1 - late
        unit, at = spot(offset_of(way, hop - 1), half)
        next_unit, next_at = spot(offset_of(way, hop), half)
        number = (hop - 1) * 2 + late
        return remote(
            xg.at[unit, 0, at], xg.at[next_unit, 0, next_at],
            ag_s.at[way, number], ag_r.at[way, number], toward[way],
        )

    def sibling_x(unit, way):
        number = unit * 2 + way
        return remote(
            xg.at[unit, 0, way], xg.at[unit, 1, way], sx_s.at[number], sx_r.at[number], sibling
        )

    def sibling_y(unit):
        return remote(yb.at[unit, 1], ys.at[unit], sy_s.at[unit], sy_r.at[unit], sibling)

    def route_copy(way, hop):
        return remote(
            routes.at[offset_of(way, hop - 1), 0], routes.at[offset_of(way, hop), 0],
            rt_s.at[way, hop - 1], rt_r.at[way, hop - 1], toward[way],
        )

    def sibling_route(offset):
        return remote(
            routes.at[offset, 0], routes.at[offset, 1], rx_s.at[offset], rx_r.at[offset], sibling
        )

    as_float = x_ref[...].astype(jnp.float32)
    inv_rms = lax.rsqrt(jnp.mean(as_float * as_float, axis=1, keepdims=True) + 1e-06)
    normed = (as_float * inv_rms * gain_ref[...]).astype(jnp.bfloat16)
    xg[0, 0] = normed.reshape(2, half_rows, width)
    pl.semaphore_wait(barrier, 3)

    for late in range(2):
        for way in range(2):
            gather_copy(way, 1, late).start()
    for way in range(2):
        sibling_x(0, way).start()

    logits = lax.dot_general(
        router_ref[...], normed, (((1,), (1,)), ((), ())), preferred_element_type=jnp.float32
    )
    exp_logits = jnp.exp(logits)
    expert_iota = lax.broadcasted_iota(jnp.int32, logits.shape, 0)
    chosen = expert_iota < 0
    for k in range(ids_ref.shape[0]):
        chosen = chosen | (ids_ref[k : k + 1, :] == expert_iota)
    picked = jnp.where(chosen, exp_logits, 0.0)
    routes[0, 0] = picked / jnp.sum(picked, axis=0, keepdims=True)
    route_copy(0, 1).start()
    route_copy(1, 1).start()
    sibling_route(0).start()

    diagonal = lax.broadcasted_iota(jnp.int32, (rows, rows), 0) == lax.broadcasted_iota(
        jnp.int32, (rows, rows), 1
    )

    def columns_of(offset):
        sibling_route(offset).wait_recv()
        for lane in range(2):
            values = routes[offset, lane, pl.ds(me, 1), :]
            column = jnp.sum(jnp.where(diagonal, values, 0.0), axis=1, keepdims=True)
            spread = jnp.broadcast_to(column, (rows, rows))
            for half in range(2):
                unit, way = spot(offset, half)
                route_col[unit, lane, way] = spread[half * half_rows : (half + 1) * half_rows]

    def compute(unit):
        for way in range(2):
            sibling_x(unit, way).wait_recv()

        @pl.loop(0, ff // FF_TILE)
        def _(tile):
            columns = pl.ds(pl.multiple_of(tile * FF_TILE, FF_TILE), FF_TILE)
            x = xg[unit].reshape(total, width)
            gate = jnp.dot(x, gate_w[:, columns], preferred_element_type=jnp.float32)
            up = jnp.dot(x, up_w[:, columns], preferred_element_type=jnp.float32)
            hb[:, columns] = (gate / (1.0 + jnp.exp(-gate)) * up).astype(jnp.bfloat16)

        @pl.loop(0, width // OUT_TILE)
        def _(tile):
            columns = pl.ds(pl.multiple_of(tile * OUT_TILE, OUT_TILE), OUT_TILE)
            y = jnp.dot(hb[...], down_w[:, columns], preferred_element_type=jnp.float32)
            for lane in range(2):
                for way in range(2):
                    first = (lane * 2 + way) * half_rows
                    weight = route_col[unit, lane, way]
                    weight = jnp.concatenate([weight] * (OUT_TILE // rows), axis=1)
                    part = y[first : first + half_rows] * weight
                    yb[unit, lane, way, :, columns] = part.astype(jnp.bfloat16)

        sibling_y(unit).start()

    incoming = (from_left, from_right)

    def reduce_copy(way, half, hops):
        unit, at = spot(RING - hops if way == 0 else hops, half)
        number = hops * 2 + half
        return remote(
            yb.at[unit, 0, at], incoming[way].at[hops - 1, half],
            rs_s.at[way, number], rs_r.at[way, number], toward[way],
        )

    def own_sum(unit, way):
        return yb[unit, 0, way].astype(jnp.float32) + ys[unit, way].astype(jnp.float32)

    def reduce_start(way, half, hops, arrived):
        unit, at = spot(RING - hops if way == 0 else hops, half)
        value = own_sum(unit, at)
        if arrived:
            reduce_copy(way, half, hops + 1).wait_recv()
            value = value + incoming[way][hops, half].astype(jnp.float32)
        yb[unit, 0, at] = value.astype(jnp.bfloat16)
        reduce_copy(way, half, hops).start()

    for hop in range(1, 4):
        for way in range(2):
            gather_copy(way, hop, 0).wait_recv()
            gather_copy(way, hop + 1, 0).start()
            sibling_x(2 * hop - 1, way).start()
        for way in range(2):
            route_copy(way, hop).wait_recv()
            if way == 0 or hop < 3:
                route_copy(way, hop + 1).start()
            sibling_route(offset_of(way, hop)).start()
        if hop == 1:
            columns_of(0)
            for load in loads:
                load.wait()
        compute(2 * hop - 2)
        columns_of(hop)
        columns_of(RING - hop)
        if hop == 3:
            compute(5)
        for way in range(2):
            gather_copy(way, hop, 1).wait_recv()
            if hop < 3:
                gather_copy(way, hop + 1, 1).start()
            sibling_x(2 * hop, way).start()
        if hop < 3:
            compute(2 * hop - 1)

    route_copy(0, 4).wait_recv()
    sibling_route(4).start()
    for unit in range(6):
        sibling_y(unit).wait_recv()
    reduce_start(0, 1, 3, False)
    reduce_start(1, 0, 3, False)
    for way in range(2):
        gather_copy(way, 4, 0).wait_recv()
        sibling_x(7, way).start()
    columns_of(4)
    compute(7)
    sibling_y(7).wait_recv()
    reduce_start(0, 0, 4, False)
    reduce_start(1, 1, 4, False)
    reduce_start(0, 1, 2, True)
    reduce_start(1, 0, 2, True)
    compute(6)
    sibling_y(6).wait_recv()
    for late, hops in ((1, 3), (0, 1), (1, 2), (1, 1)):
        reduce_start(0, 1 - late, hops, True)
        reduce_start(1, late, hops, True)

    def out_copy(half):
        return pltpu.make_async_copy(
            out_buf.at[half], out_ref.at[pl.ds(half * half_rows, half_rows)], out_sem.at[half]
        )

    for half in range(2):
        value = own_sum(0, half)
        for way in range(2):
            reduce_copy(way, half, 1).wait_recv()
            value = value + incoming[way][0, half].astype(jnp.float32)
        out_buf[half] = value.astype(jnp.bfloat16)
        out_copy(half).start()

    for way in range(2):
        for hop in range(1, 5):
            for late in range(2 if hop < 4 else 1):
                gather_copy(way, hop, late).wait_send()
            if way == 0 or hop < 4:
                route_copy(way, hop).wait_send()
        for hops in (1, 2, 3):
            for half in range(2):
                reduce_copy(way, half, hops).wait_send()
        reduce_copy(way, way, 4).wait_send()
    for unit in range(RING):
        for way in range(2):
            sibling_x(unit, way).wait_send()
        sibling_y(unit).wait_send()
        sibling_route(unit).wait_send()
    for half in range(2):
        out_copy(half).wait()


def ring_local(hidden_in, norm_gain, router_weight, expert_ids, w_gate, w_up, w_down):
    rows, width = hidden_in.shape
    ff = w_gate.shape[2]
    half = rows // 2
    count = router_weight.shape[1]
    vmem = pl.BlockSpec(memory_space=pltpu.VMEM)
    hbm = pl.BlockSpec(memory_space=pl.ANY)
    dma = pltpu.SemaphoreType.DMA
    return pl.pallas_call(
        ring_kernel,
        out_shape=jax.ShapeDtypeStruct((rows, width), jnp.bfloat16),
        in_specs=[vmem, vmem, vmem, vmem, hbm, hbm, hbm],
        out_specs=hbm,
        scratch_shapes=[
            pltpu.VMEM((width, ff), jnp.bfloat16),
            pltpu.VMEM((width, ff), jnp.bfloat16),
            pltpu.VMEM((ff, width), jnp.bfloat16),
            pltpu.VMEM((RING, 2, 2, half, width), jnp.bfloat16),
            pltpu.VMEM((RING, 2, 2, half, width), jnp.bfloat16),
            pltpu.VMEM((RING, 2, half, width), jnp.bfloat16),
            pltpu.VMEM((4, 2, half, width), jnp.bfloat16),
            pltpu.VMEM((4, 2, half, width), jnp.bfloat16),
            pltpu.VMEM((2 * rows, ff), jnp.bfloat16),
            pltpu.VMEM((RING, 2, count, rows), jnp.float32),
            pltpu.VMEM((RING, 2, 2, half, rows), jnp.float32),
            pltpu.VMEM((2, half, width), jnp.bfloat16),
            dma((3,)), dma((2, 8)), dma((2, 8)), dma((2 * RING,)), dma((2 * RING,)),
            dma((RING,)), dma((RING,)), dma((2, 10)), dma((2, 10)), dma((2, 4)), dma((2, 4)),
            dma((RING,)), dma((RING,)), dma((2,)),
        ],
        compiler_params=pltpu.CompilerParams(
            collective_id=0, has_side_effects=True, vmem_limit_bytes=56 * 1024 * 1024
        ),
    )(hidden_in, norm_gain.reshape(1, width), router_weight.T, expert_ids.T, w_gate, w_up, w_down)


def local(hidden_in, norm_gain, router_weight, expert_ids, w_gate, w_up, w_down):
    tok_rows = hidden_in.shape[0]
    top_count = expert_ids.shape[1]
    num_experts = router_weight.shape[1]
    dev_count = lax.axis_size("expert")
    local_experts = w_gate.shape[0]
    cap_rows = tok_rows * top_count * 3 // (2 * num_experts)
    as_float = hidden_in.astype(jnp.float32)
    inv_rms = lax.rsqrt(jnp.mean(as_float * as_float, axis=1, keepdims=True) + 1e-06)
    normed = (as_float * inv_rms * norm_gain).astype(jnp.bfloat16)
    logits = jnp.dot(normed, router_weight, preferred_element_type=jnp.float32)
    exp_logits = jnp.exp(logits)
    expert_iota = jnp.arange(num_experts, dtype=jnp.int32)
    choice_hot = (expert_ids[:, :, None] == expert_iota[None, None, :]).astype(jnp.float32)
    picked = jnp.sum(choice_hot * exp_logits[:, None, :], axis=2)
    route_w = picked / jnp.sum(picked, axis=1, keepdims=True)
    flat_ids = expert_ids.reshape(-1)
    onehot = (flat_ids[:, None] == expert_iota[None, :]).astype(jnp.int32)
    before = jnp.cumsum(onehot, axis=0) - onehot
    slot_index = jnp.sum(before * onehot, axis=1)
    dest_index = (
        flat_ids // local_experts * cap_rows + slot_index
    ) * local_experts + flat_ids % local_experts
    token_rows = jnp.repeat(normed, top_count, axis=0)
    outgoing = (
        jnp.zeros((num_experts * cap_rows, normed.shape[1]), jnp.bfloat16)
        .at[dest_index]
        .set(token_rows)
    )
    outgoing = outgoing.reshape(dev_count, cap_rows, local_experts, normed.shape[1])
    arrived = lax.all_to_all(outgoing, "expert", split_axis=0, concat_axis=0, tiled=True)
    gate_act = jnp.einsum("smed,edf->smef", arrived, w_gate, preferred_element_type=jnp.float32)
    up_act = jnp.einsum("smed,edf->smef", arrived, w_up, preferred_element_type=jnp.float32)
    hidden = (jax.nn.silu(gate_act) * up_act).astype(jnp.bfloat16)
    returned = lax.all_to_all(
        jnp.einsum("smef,efd->smed", hidden, w_down, preferred_element_type=jnp.float32).astype(
            jnp.bfloat16
        ),
        "expert",
        split_axis=0,
        concat_axis=0,
        tiled=True,
    )
    returned = returned.reshape(num_experts * cap_rows, normed.shape[1])
    gathered = returned[dest_index].reshape(tok_rows, top_count, normed.shape[1])
    combined = jnp.sum(gathered.astype(jnp.float32) * route_w[:, :, None], axis=1).astype(
        jnp.bfloat16
    )
    return combined


def solution(mesh):
    in_specs = (
        P(("groups", "expert"), None),
        P(),
        P(),
        P(("groups", "expert"), None),
        P("expert", None, None),
        P("expert", None, None),
        P("expert", None, None),
    )
    out_specs = P(("groups", "expert"), None)
    ringed = mesh.shape["expert"] == 2 * RING
    body = ring_local if ringed else local
    return jax.shard_map(body, mesh=mesh, in_specs=in_specs, out_specs=out_specs, check_vma=False)
```

```python
import jax
import jax.numpy as jnp
from jax import lax
from jax.experimental import pallas as pl
from jax.experimental.pallas import tpu as pltpu
from jax.sharding import PartitionSpec as P

RING = 8
FF_TILE = 768
OUT_TILE = 2048


def spot(offset, half):
    if offset == 0:
        return 0, half
    if offset == 4:
        return 7, half
    if offset < 4:
        return 2 * offset - 1 + half, 0
    return 2 * (RING - offset) - half, 1


def ring_kernel(
    x_ref, gain_ref, router_ref, ids_ref, gate_hbm, up_hbm, down_hbm, out_ref,
    gate_w, up_w, down_w, xg, yb, ys, from_left, from_right, hb, routes, route_col, out_buf,
    load_sem, ag_s, ag_r, sx_s, sx_r, sy_s, sy_r, rs_s, rs_r, rt_s, rt_r, rx_s, rx_r, out_sem,
):
    rows = x_ref.shape[0]
    width = x_ref.shape[1]
    ff = gate_w.shape[1]
    half_rows = rows // 2
    total = 2 * rows
    me = lax.axis_index("expert")
    core = me % 2
    y_at = (me // 2) % 2
    z_at = me // 4
    place = z_at * (1 - y_at) + (RING - 1 - z_at) * y_at

    def device_at(ring_place):
        high = ring_place // 4
        depth = ring_place * (1 - high) + (RING - 1 - ring_place) * high
        return (depth * 2 + high) * 2 + core

    right = device_at((place + 1) % RING)
    left = device_at((place + RING - 1) % RING)
    sibling = me + 1 - 2 * core
    toward = (right, left)

    barrier = pltpu.get_barrier_semaphore()
    for device in (right, left, sibling):
        pl.semaphore_signal(
            barrier, inc=1, device_id={"expert": device}, device_id_type=pl.DeviceIdType.MESH
        )

    loads = [
        pltpu.make_async_copy(src.at[0], dst, load_sem.at[i])
        for i, (src, dst) in enumerate(((gate_hbm, gate_w), (up_hbm, up_w), (down_hbm, down_w)))
    ]

    def remote(src, dst, send, recv, device):
        return pltpu.make_async_remote_copy(
            src_ref=src, dst_ref=dst, send_sem=send, recv_sem=recv,
            device_id={"expert": device}, device_id_type=pl.DeviceIdType.MESH,
        )

    def offset_of(way, hop):
        return hop if way == 0 else (RING - hop) % RING

    def gather_copy(way, hop, late):
        half = late if way == 0 else 1 - late
        unit, at = spot(offset_of(way, hop - 1), half)
        next_unit, next_at = spot(offset_of(way, hop), half)
        number = (hop - 1) * 2 + late
        return remote(
            xg.at[unit, 0, at], xg.at[next_unit, 0, next_at],
            ag_s.at[way, number], ag_r.at[way, number], toward[way],
        )

    def sibling_x(unit, way):
        number = unit * 2 + way
        return remote(
            xg.at[unit, 0, way], xg.at[unit, 1, way], sx_s.at[number], sx_r.at[number], sibling
        )

    def sibling_y(unit):
        return remote(yb.at[unit, 1], ys.at[unit], sy_s.at[unit], sy_r.at[unit], sibling)

    def route_copy(way, hop):
        return remote(
            routes.at[offset_of(way, hop - 1), 0], routes.at[offset_of(way, hop), 0],
            rt_s.at[way, hop - 1], rt_r.at[way, hop - 1], toward[way],
        )

    def sibling_route(offset):
        return remote(
            routes.at[offset, 0], routes.at[offset, 1], rx_s.at[offset], rx_r.at[offset], sibling
        )

    as_float = x_ref[...].astype(jnp.float32)
    inv_rms = lax.rsqrt(jnp.mean(as_float * as_float, axis=1, keepdims=True) + 1e-06)
    normed = (as_float * inv_rms * gain_ref[...]).astype(jnp.bfloat16)
    xg[0, 0] = normed.reshape(2, half_rows, width)
    pl.semaphore_wait(barrier, 3)

    for late in range(2):
        for way in range(2):
            gather_copy(way, 1, late).start()
    for way in range(2):
        sibling_x(0, way).start()
    for load in loads:
        load.start()

    logits = lax.dot_general(
        router_ref[...], normed, (((1,), (1,)), ((), ())), preferred_element_type=jnp.float32
    )
    exp_logits = jnp.exp(logits)
    expert_iota = lax.broadcasted_iota(jnp.int32, logits.shape, 0)
    chosen = expert_iota < 0
    for k in range(ids_ref.shape[0]):
        chosen = chosen | (ids_ref[k : k + 1, :] == expert_iota)
    picked = jnp.where(chosen, exp_logits, 0.0)
    routes[0, 0] = picked / jnp.sum(picked, axis=0, keepdims=True)
    route_copy(0, 1).start()
    route_copy(1, 1).start()
    sibling_route(0).start()

    diagonal = lax.broadcasted_iota(jnp.int32, (rows, rows), 0) == lax.broadcasted_iota(
        jnp.int32, (rows, rows), 1
    )

    def columns_of(offset):
        sibling_route(offset).wait_recv()
        for lane in range(2):
            values = routes[offset, lane, pl.ds(me, 1), :]
            column = jnp.sum(jnp.where(diagonal, values, 0.0), axis=1, keepdims=True)
            spread = jnp.broadcast_to(column, (rows, rows))
            for half in range(2):
                unit, way = spot(offset, half)
                route_col[unit, lane, way] = spread[half * half_rows : (half + 1) * half_rows]

    def compute(unit):
        for way in range(2):
            sibling_x(unit, way).wait_recv()

        @pl.loop(0, ff // FF_TILE)
        def _(tile):
            columns = pl.ds(pl.multiple_of(tile * FF_TILE, FF_TILE), FF_TILE)
            x = xg[unit].reshape(total, width)
            gate = jnp.dot(x, gate_w[:, columns], preferred_element_type=jnp.float32)
            up = jnp.dot(x, up_w[:, columns], preferred_element_type=jnp.float32)
            hb[:, columns] = (gate / (1.0 + jnp.exp(-gate)) * up).astype(jnp.bfloat16)

        @pl.loop(0, width // OUT_TILE)
        def _(tile):
            columns = pl.ds(pl.multiple_of(tile * OUT_TILE, OUT_TILE), OUT_TILE)
            y = jnp.dot(hb[...], down_w[:, columns], preferred_element_type=jnp.float32)
            for lane in range(2):
                for way in range(2):
                    first = (lane * 2 + way) * half_rows
                    weight = route_col[unit, lane, way]
                    weight = jnp.concatenate([weight] * (OUT_TILE // rows), axis=1)
                    part = y[first : first + half_rows] * weight
                    yb[unit, lane, way, :, columns] = part.astype(jnp.bfloat16)

        sibling_y(unit).start()

    incoming = (from_left, from_right)

    def reduce_copy(way, half, hops):
        unit, at = spot(RING - hops if way == 0 else hops, half)
        number = hops * 2 + half
        return remote(
            yb.at[unit, 0, at], incoming[way].at[hops - 1, half],
            rs_s.at[way, number], rs_r.at[way, number], toward[way],
        )

    def own_sum(unit, way):
        return yb[unit, 0, way].astype(jnp.float32) + ys[unit, way].astype(jnp.float32)

    def reduce_start(way, half, hops, arrived):
        unit, at = spot(RING - hops if way == 0 else hops, half)
        value = own_sum(unit, at)
        if arrived:
            reduce_copy(way, half, hops + 1).wait_recv()
            value = value + incoming[way][hops, half].astype(jnp.float32)
        yb[unit, 0, at] = value.astype(jnp.bfloat16)
        reduce_copy(way, half, hops).start()

    for hop in range(1, 4):
        for way in range(2):
            gather_copy(way, hop, 0).wait_recv()
            gather_copy(way, hop + 1, 0).start()
            sibling_x(2 * hop - 1, way).start()
        for way in range(2):
            route_copy(way, hop).wait_recv()
            if way == 0 or hop < 3:
                route_copy(way, hop + 1).start()
            sibling_route(offset_of(way, hop)).start()
        if hop == 1:
            columns_of(0)
            for load in loads:
                load.wait()
        compute(2 * hop - 2)
        columns_of(hop)
        columns_of(RING - hop)
        if hop == 3:
            compute(5)
        for way in range(2):
            gather_copy(way, hop, 1).wait_recv()
            if hop < 3:
                gather_copy(way, hop + 1, 1).start()
            sibling_x(2 * hop, way).start()
        if hop < 3:
            compute(2 * hop - 1)

    route_copy(0, 4).wait_recv()
    sibling_route(4).start()
    for unit in range(6):
        sibling_y(unit).wait_recv()
    reduce_start(0, 1, 3, False)
    reduce_start(1, 0, 3, False)
    for way in range(2):
        gather_copy(way, 4, 0).wait_recv()
        sibling_x(7, way).start()
    columns_of(4)
    compute(7)
    reduce_start(0, 1, 2, True)
    reduce_start(1, 0, 2, True)
    sibling_y(7).wait_recv()
    reduce_start(0, 0, 4, False)
    reduce_start(1, 1, 4, False)
    compute(6)
    sibling_y(6).wait_recv()
    for late, hops in ((1, 3), (0, 1), (1, 2), (1, 1)):
        reduce_start(0, 1 - late, hops, True)
        reduce_start(1, late, hops, True)

    def out_copy(half):
        return pltpu.make_async_copy(
            out_buf.at[half], out_ref.at[pl.ds(half * half_rows, half_rows)], out_sem.at[half]
        )

    for half in range(2):
        value = own_sum(0, half)
        for way in range(2):
            reduce_copy(way, half, 1).wait_recv()
            value = value + incoming[way][0, half].astype(jnp.float32)
        out_buf[half] = value.astype(jnp.bfloat16)
        out_copy(half).start()

    for way in range(2):
        for hop in range(1, 5):
            for late in range(2 if hop < 4 else 1):
                gather_copy(way, hop, late).wait_send()
            if way == 0 or hop < 4:
                route_copy(way, hop).wait_send()
        for hops in (1, 2, 3):
            for half in range(2):
                reduce_copy(way, half, hops).wait_send()
        reduce_copy(way, way, 4).wait_send()
    for unit in range(RING):
        for way in range(2):
            sibling_x(unit, way).wait_send()
        sibling_y(unit).wait_send()
        sibling_route(unit).wait_send()
    for half in range(2):
        out_copy(half).wait()


def ring_local(hidden_in, norm_gain, router_weight, expert_ids, w_gate, w_up, w_down):
    rows, width = hidden_in.shape
    ff = w_gate.shape[2]
    half = rows // 2
    count = router_weight.shape[1]
    vmem = pl.BlockSpec(memory_space=pltpu.VMEM)
    hbm = pl.BlockSpec(memory_space=pl.ANY)
    dma = pltpu.SemaphoreType.DMA
    return pl.pallas_call(
        ring_kernel,
        out_shape=jax.ShapeDtypeStruct((rows, width), jnp.bfloat16),
        in_specs=[vmem, vmem, vmem, vmem, hbm, hbm, hbm],
        out_specs=hbm,
        scratch_shapes=[
            pltpu.VMEM((width, ff), jnp.bfloat16),
            pltpu.VMEM((width, ff), jnp.bfloat16),
            pltpu.VMEM((ff, width), jnp.bfloat16),
            pltpu.VMEM((RING, 2, 2, half, width), jnp.bfloat16),
            pltpu.VMEM((RING, 2, 2, half, width), jnp.bfloat16),
            pltpu.VMEM((RING, 2, half, width), jnp.bfloat16),
            pltpu.VMEM((4, 2, half, width), jnp.bfloat16),
            pltpu.VMEM((4, 2, half, width), jnp.bfloat16),
            pltpu.VMEM((2 * rows, ff), jnp.bfloat16),
            pltpu.VMEM((RING, 2, count, rows), jnp.float32),
            pltpu.VMEM((RING, 2, 2, half, rows), jnp.float32),
            pltpu.VMEM((2, half, width), jnp.bfloat16),
            dma((3,)), dma((2, 8)), dma((2, 8)), dma((2 * RING,)), dma((2 * RING,)),
            dma((RING,)), dma((RING,)), dma((2, 10)), dma((2, 10)), dma((2, 4)), dma((2, 4)),
            dma((RING,)), dma((RING,)), dma((2,)),
        ],
        compiler_params=pltpu.CompilerParams(
            collective_id=0, has_side_effects=True, vmem_limit_bytes=56 * 1024 * 1024
        ),
    )(hidden_in, norm_gain.reshape(1, width), router_weight.T, expert_ids.T, w_gate, w_up, w_down)


def local(hidden_in, norm_gain, router_weight, expert_ids, w_gate, w_up, w_down):
    tok_rows = hidden_in.shape[0]
    top_count = expert_ids.shape[1]
    num_experts = router_weight.shape[1]
    dev_count = lax.axis_size("expert")
    local_experts = w_gate.shape[0]
    cap_rows = tok_rows * top_count * 3 // (2 * num_experts)
    as_float = hidden_in.astype(jnp.float32)
    inv_rms = lax.rsqrt(jnp.mean(as_float * as_float, axis=1, keepdims=True) + 1e-06)
    normed = (as_float * inv_rms * norm_gain).astype(jnp.bfloat16)
    logits = jnp.dot(normed, router_weight, preferred_element_type=jnp.float32)
    exp_logits = jnp.exp(logits)
    expert_iota = jnp.arange(num_experts, dtype=jnp.int32)
    choice_hot = (expert_ids[:, :, None] == expert_iota[None, None, :]).astype(jnp.float32)
    picked = jnp.sum(choice_hot * exp_logits[:, None, :], axis=2)
    route_w = picked / jnp.sum(picked, axis=1, keepdims=True)
    flat_ids = expert_ids.reshape(-1)
    onehot = (flat_ids[:, None] == expert_iota[None, :]).astype(jnp.int32)
    before = jnp.cumsum(onehot, axis=0) - onehot
    slot_index = jnp.sum(before * onehot, axis=1)
    dest_index = (
        flat_ids // local_experts * cap_rows + slot_index
    ) * local_experts + flat_ids % local_experts
    token_rows = jnp.repeat(normed, top_count, axis=0)
    outgoing = (
        jnp.zeros((num_experts * cap_rows, normed.shape[1]), jnp.bfloat16)
        .at[dest_index]
        .set(token_rows)
    )
    outgoing = outgoing.reshape(dev_count, cap_rows, local_experts, normed.shape[1])
    arrived = lax.all_to_all(outgoing, "expert", split_axis=0, concat_axis=0, tiled=True)
    gate_act = jnp.einsum("smed,edf->smef", arrived, w_gate, preferred_element_type=jnp.float32)
    up_act = jnp.einsum("smed,edf->smef", arrived, w_up, preferred_element_type=jnp.float32)
    hidden = (jax.nn.silu(gate_act) * up_act).astype(jnp.bfloat16)
    returned = lax.all_to_all(
        jnp.einsum("smef,efd->smed", hidden, w_down, preferred_element_type=jnp.float32).astype(
            jnp.bfloat16
        ),
        "expert",
        split_axis=0,
        concat_axis=0,
        tiled=True,
    )
    returned = returned.reshape(num_experts * cap_rows, normed.shape[1])
    gathered = returned[dest_index].reshape(tok_rows, top_count, normed.shape[1])
    combined = jnp.sum(gathered.astype(jnp.float32) * route_w[:, :, None], axis=1).astype(
        jnp.bfloat16
    )
    return combined


def solution(mesh):
    in_specs = (
        P(("groups", "expert"), None),
        P(),
        P(),
        P(("groups", "expert"), None),
        P("expert", None, None),
        P("expert", None, None),
        P("expert", None, None),
    )
    out_specs = P(("groups", "expert"), None)
    ringed = mesh.shape["expert"] == 2 * RING
    body = ring_local if ringed else local
    return jax.shard_map(body, mesh=mesh, in_specs=in_specs, out_specs=out_specs, check_vma=False)
```
